32 devices in a mesh: dp: 16 (over z, x, core), tile: 2 (over y).
Axes of the slice: x: 2, y: 2, z: 4, core: 2. Of those that a mesh axis runs over, the one named last changes fastest.
Arguments:
- proposal_boxes: int32 [16, 4, 512], P('dp'), may hold values from 0 to 672, as said below
- level_plan: int32 [16, 512], P('dp'), may hold values from 0 to 1
- fine_map: bfloat16 [16, 84, 168, 128], P('dp', 'tile'), may hold values from -6 to 6
- coarse_map: bfloat16 [16, 42, 84, 128], P('dp', 'tile'), may hold values from -6 to 6
- first_weight: bfloat16 [6272, 1024], P('tile', 'dp'), may hold values from -0.078125 to 0.078125
- second_weight: bfloat16 [1024, 1024], P('tile', 'dp'), may hold values from -0.1875 to 0.1875
- upstream: bfloat16 [16, 512, 1024], P('dp'), may hold values from -6 to 6
Outputs:
- first_grad: float32 [6272, 1024], P('tile', 'dp')
- second_grad: float32 [1024, 1024], P('tile', 'dp')
The draws below stay inside these ranges and needn't reach their ends.
Inputs may be any that keep to these rules, and one draw needn't show every extreme that they name: `proposal_boxes`: with s = 4 where level_plan is 0 and s = 8 where it is 1: h >= 1, w >= 1, y0 + h <= 336, x0 + w <= 672, (y0 mod s) + h <= 14 * s and (x0 mod s) + w <= 14 * s. Band b holds the proposals with b * 168 <= y0 < (b + 1) * 168; at most 256 of an image's proposals lie in one band, and in every image some band holds exactly 256.
All inputs are finite; a program needn't handle non-finite values.
Results may differ from the reference program's by a relative error of at most 0.017.
Values may be sent and summed in bfloat16 or wider, within the bound.
A program may use at most 64 MiB of HBM per device.

```python
import jax
import jax.numpy as jnp
from jax import lax

CH = 128
HIDDEN_SIZE = 1024
FEATS = 6272
WIN = 16
ROWS2 = 42
COLS2 = 168
ROWS3 = 21
COLS3 = 84
PROPS = 512
CAP = 256
IMAGES = 16
BAND_PX = 168
HEIGHT_PX = 336
WIDTH_PX = 672
N_TILE = 2


def proposal_plan(key):
    base_key = jax.random.fold_in(key, 11)
    key_level, key_busy, key_order, key_top, key_height, key_left, key_width = jax.random.split(base_key, 7)
    grid_shape = (IMAGES, PROPS)
    level_draw = jax.random.randint(key_level, grid_shape, 0, 2)
    busy_band = jax.random.randint(key_busy, (IMAGES, 1), 0, N_TILE)
    slot_index = jnp.arange(PROPS)[None, :]
    other_bands = max(N_TILE - 1, 1)
    spread_band = (busy_band + 1 + jnp.maximum(slot_index - CAP, 0) % other_bands) % N_TILE
    listed_band = jnp.where(slot_index < CAP, busy_band, spread_band)
    shuffles = jax.vmap(lambda order_key: jax.random.permutation(order_key, PROPS))(jax.random.split(key_order, IMAGES))
    owner_band = jnp.take_along_axis(listed_band, shuffles, axis=1)
    stride = jnp.where(level_draw == 0, 4, 8)
    top_pixel = owner_band * BAND_PX + jax.random.randint(key_top, grid_shape, 0, BAND_PX)
    height_most = jnp.minimum(14 * stride - top_pixel % stride, HEIGHT_PX - top_pixel)
    height_draw = jax.random.randint(key_height, grid_shape, jnp.minimum(stride, height_most), height_most + 1)
    left_pixel = jax.random.randint(key_left, grid_shape, 0, WIDTH_PX)
    width_most = jnp.minimum(14 * stride - left_pixel % stride, WIDTH_PX - left_pixel)
    width_draw = jax.random.randint(key_width, grid_shape, jnp.minimum(stride, width_most), width_most + 1)
    box_array = jnp.stack([top_pixel, left_pixel, height_draw, width_draw], axis=1).astype(jnp.int32)
    return (box_array, level_draw.astype(jnp.int32))


def draw_proposal_boxes(key, part):
    return proposal_plan(key)[0]


def draw_level_plan(key, part):
    return proposal_plan(key)[1]


def block_scale(stream_key, shape, shards, low, high):
    gain, own = 1.0, jax.random.fold_in(stream_key, 6)
    for axis_at, shards_of in shards:
        draws = jnp.exp(jax.random.uniform(jax.random.fold_in(own, axis_at), (shards_of,), jnp.float32, low / len(shards), high / len(shards)))
        gain = gain * jnp.repeat(draws, shape[axis_at] // shards_of).reshape([-1 if axis == axis_at else 1 for axis in range(len(shape))])
    return gain


def gaussian(own_key, dims, scale, limit, cuts=(), held_as=jnp.bfloat16):
    entries = jax.random.normal(own_key, dims, jnp.float32) * scale
    if len(cuts) > 0:
        entries = block_scale(own_key, dims, cuts, -0.22, 0.18) * entries
    return jnp.clip(entries, min=-limit, max=limit).astype(held_as)


def setup_inputs(seed: int = 0) -> dict:
    key_of = jax.random.split(jax.random.key(seed), 8)
    proposal_boxes = draw_proposal_boxes(jax.random.fold_in(key_of[7], 71), 0)
    level_plan = draw_level_plan(jax.random.fold_in(key_of[7], 71), 0)
    fine_map = gaussian(key_of[2], (IMAGES, ROWS2 * N_TILE, COLS2, CH), 1.0, 6.0, ((0, 16), (1, 2)))
    coarse_map = gaussian(key_of[3], (IMAGES, ROWS3 * N_TILE, COLS3, CH), 1.0, 6.0, ((0, 16), (1, 2)))
    first_weight = gaussian(key_of[4], (FEATS, HIDDEN_SIZE), FEATS ** -0.5, 0.078125, ((0, 2), (1, 16)))
    second_weight = gaussian(key_of[5], (HIDDEN_SIZE, HIDDEN_SIZE), HIDDEN_SIZE ** -0.5, 0.1875, ((0, 2), (1, 16)))
    upstream = gaussian(key_of[6], (IMAGES, PROPS, HIDDEN_SIZE), 1.0, 6.0, ((0, 16),))
    return {"proposal_boxes": proposal_boxes, "level_plan": level_plan, "fine_map": fine_map, "coarse_map": coarse_map, "first_weight": first_weight, "second_weight": second_weight, "upstream": upstream}


def gelu_parts(hidden):
    factor = 0.7978845608028654
    cubic_term = 0.044715
    inner_term = factor * (hidden + cubic_term * hidden * hidden * hidden)
    tangent = jnp.tanh(inner_term)
    gelu_value = 0.5 * hidden * (1.0 + tangent)
    gelu_slope = 0.5 * (1.0 + tangent) + 0.5 * hidden * (1.0 - tangent * tangent) * factor * (1.0 + 3.0 * cubic_term * hidden * hidden)
    return gelu_value, gelu_slope


def block_size(num_items):
    return 32 if num_items % 32 == 0 else num_items


def axis_weights(begin_px, extent, first_cell, stride):
    stride_float = stride.astype(jnp.float32)[:, None]
    bin_index = jnp.arange(7, dtype=jnp.float32)[None, :]
    sample_pos = begin_px.astype(jnp.float32)[:, None] / stride_float + (bin_index + 0.5) * extent.astype(jnp.float32)[:, None] / (7.0 * stride_float)
    cell_pos = first_cell.astype(jnp.float32)[:, None, None] + jnp.arange(WIN, dtype=jnp.float32)[None, None, :]
    return jnp.maximum(0.0, 1.0 - jnp.abs(sample_pos[:, :, None] - cell_pos))


def crop_block(combined, fields, levels_blk, shift_fine, shift_coarse, limit_fine, limit_coarse, offset):
    top_pixel = fields[0]
    left_pixel = fields[1]
    height = fields[2]
    box_width = fields[3]
    stride = jnp.where(levels_blk == 0, 4, 8).astype(jnp.int32)
    first_row = (top_pixel // stride).astype(jnp.int32)
    first_col = jnp.minimum(left_pixel // stride, jnp.where(levels_blk == 0, limit_fine, limit_coarse) - WIN).astype(jnp.int32)
    start_row = jnp.where(levels_blk == 0, first_row - shift_fine, offset + first_row - shift_coarse).astype(jnp.int32)
    channels = combined.shape[2]
    zero_index = jnp.zeros((), jnp.int32)

    def window(row_start, col_start):
        return lax.dynamic_slice(combined, (row_start.astype(jnp.int32), col_start.astype(jnp.int32), zero_index), (WIN, WIN, channels))

    windows = jax.vmap(window)(start_row, first_col).astype(jnp.float32)
    row_low = lax.optimization_barrier(axis_weights(top_pixel, height, first_row, stride).astype(jnp.bfloat16))
    col_low = lax.optimization_barrier(axis_weights(left_pixel, box_width, first_col, stride).astype(jnp.bfloat16))
    row_weights = row_low.astype(jnp.float32)
    col_weights = col_low.astype(jnp.float32)
    partial_rows = jnp.einsum("bia,baqc->biqc", row_weights, windows, precision=lax.Precision.HIGHEST)
    crop_rows = jnp.einsum("bjq,biqc->bijc", col_weights, partial_rows, precision=lax.Precision.HIGHEST)
    return crop_rows.reshape(crop_rows.shape[0], 49 * channels).astype(jnp.bfloat16)


def image_crops(inputs):
    fields, levels_img, fine_tile, coarse = inputs
    fine_rows, fine_cols, channels = fine_tile.shape
    coarse_cols = coarse.shape[1]
    fine_pad = jnp.pad(fine_tile, ((0, WIN), (0, WIN), (0, 0)))
    coarse_pad = jnp.pad(coarse, ((0, WIN), (0, fine_cols + WIN - coarse_cols), (0, 0)))
    combined = jnp.concatenate([fine_pad, coarse_pad], axis=0)
    num_props = levels_img.shape[0]
    block_len = block_size(num_props)
    grouped_fields = fields.reshape(4, num_props // block_len, block_len).transpose(1, 0, 2)
    grouped_levels = levels_img.reshape(num_props // block_len, block_len)

    def crop_group(pieces):
        part_fields, part_levels = pieces
        return crop_block(combined, part_fields, part_levels, 0, 0, fine_cols + WIN, coarse_cols + WIN, fine_rows + WIN)

    grouped = lax.map(crop_group, (grouped_fields, grouped_levels))
    return grouped.reshape(num_props, 49 * channels)


def reference(proposal_boxes, level_plan, fine_map, coarse_map, first_weight, second_weight, upstream):
    crop_all = lax.map(image_crops, (proposal_boxes, level_plan, fine_map, coarse_map))
    flat_crops = crop_all.reshape(-1, crop_all.shape[2])
    upstream_rows = upstream.reshape(-1, upstream.shape[2])
    hidden = jnp.dot(flat_crops, first_weight, preferred_element_type=jnp.float32)
    gelu_value, gelu_slope = gelu_parts(hidden)
    activated = gelu_value.astype(jnp.bfloat16)
    second_grad = jnp.dot(activated.T, upstream_rows, preferred_element_type=jnp.float32)
    back_grad = jnp.dot(upstream_rows, second_weight.T, preferred_element_type=jnp.float32)
    pre_grad = (back_grad * gelu_slope).astype(jnp.bfloat16)
    first_grad = jnp.dot(flat_crops.T, pre_grad, preferred_element_type=jnp.float32)
    return first_grad, second_grad
```

```python
import functools

import jax
import jax.numpy as jnp
from jax import lax
from jax.experimental import pallas as pl
from jax.experimental.pallas import tpu as pltpu
from jax.sharding import PartitionSpec as P

WIN = 16
BINS = 7
ROWS_PAD = 56
GROUP = 16


def from_ahead(block, axis, distance):
    if distance == 0:
        return block
    size = lax.axis_size(axis)
    return lax.ppermute(block, axis, [(i, (i - distance) % size) for i in range(size)])


def halo_from_next(block, axis):
    size = lax.axis_size(axis)
    return lax.ppermute(block, axis, [(i + 1, i) for i in range(size - 1)])


def gelu_parts(hidden):
    factor = 0.7978845608028654
    cubic_term = 0.044715
    inner_term = factor * (hidden + cubic_term * hidden * hidden * hidden)
    tangent = jnp.tanh(inner_term)
    gelu_value = 0.5 * hidden * (1.0 + tangent)
    gelu_slope = 0.5 * (1.0 + tangent) + 0.5 * hidden * (1.0 - tangent * tangent) * factor * (
        1.0 + 3.0 * cubic_term * hidden * hidden
    )
    return (gelu_value, gelu_slope)


def crop_kernel(starts, width, cells_ref, geo_ref, maps_ref, out_ref, wide, stage):
    step = pl.program_id(0)

    @pl.when(step == 0)
    def _():
        def widen(r, carry):
            wide[r] = maps_ref[r].astype(jnp.float32)
            return carry

        lax.fori_loop(0, maps_ref.shape[0], widen, 0)

    shape = (ROWS_PAD, WIN * WIN)
    k = lax.broadcasted_iota(jnp.int32, shape, 0).astype(jnp.float32)
    i_bin = jnp.floor((k + 0.5) * (1.0 / BINS))
    j_bin = k - BINS * i_bin
    i_mid = i_bin + 0.5
    j_mid = j_bin + 0.5
    lane = lax.broadcasted_iota(jnp.int32, shape, 1)
    r_cell = (lane >> 4).astype(jnp.float32)
    q_cell = (lane & 15).astype(jnp.float32)
    for p in range(GROUP):
        n = step * GROUP + p
        row = cells_ref[0, n]
        col = cells_ref[1, n]
        row_w = jnp.maximum(0.0, 1.0 - jnp.abs(i_mid * geo_ref[1, n] + geo_ref[0, n] - r_cell))
        col_w = jnp.maximum(0.0, 1.0 - jnp.abs(j_mid * geo_ref[3, n] + geo_ref[2, n] - q_cell))
        weights = (row_w * col_w).astype(jnp.bfloat16)
        window = jnp.concatenate(
            [wide[row + r, pl.ds(col, WIN), :] for r in range(WIN)], axis=0
        ).astype(jnp.bfloat16)
        crop = jnp.dot(weights, window, preferred_element_type=jnp.float32)
        stage[pl.ds(p, ROWS_PAD, stride=GROUP), :] = crop
    for t, first in enumerate(starts):
        for m in range(width):
            at = (first + m) * GROUP
            out_ref[t, :, m * 128 : (m + 1) * 128] = stage[at : at + GROUP, :].astype(jnp.bfloat16)


def make_crops(cells, geo, maps, starts, width, capacity):
    tiles = len(starts)
    lanes = width * 128
    return pl.pallas_call(
        functools.partial(crop_kernel, starts, width),
        grid=(capacity // GROUP,),
        out_shape=jax.ShapeDtypeStruct((tiles, capacity, lanes), jnp.bfloat16),
        in_specs=[
            pl.BlockSpec(memory_space=pltpu.SMEM),
            pl.BlockSpec(memory_space=pltpu.SMEM),
            pl.BlockSpec(maps.shape, lambda g: (0, 0, 0)),
        ],
        out_specs=pl.BlockSpec((tiles, GROUP, lanes), lambda g: (0, g, 0)),
        scratch_shapes=[
            pltpu.VMEM(maps.shape, jnp.float32),
            pltpu.VMEM((ROWS_PAD * GROUP, 128), jnp.float32),
        ],
        compiler_params=pltpu.CompilerParams(
            dimension_semantics=("arbitrary",), vmem_limit_bytes=48 * 1024 * 1024
        ),
        cost_estimate=pl.CostEstimate(
            flops=capacity * ROWS_PAD * WIN * WIN * 128 * 16,
            bytes_accessed=2 * maps.size + 2 * tiles * capacity * lanes,
            transcendentals=0,
        ),
        name="crops",
    )(cells, geo, maps)


def per_device(
    proposal_boxes, level_plan, fine_map, coarse_map, first_weight, second_weight, upstream
):
    tile_count = lax.axis_size("tile")
    band = lax.axis_index("tile")
    num_props = level_plan.shape[1]
    capacity = max(num_props // 4, num_props // tile_count)
    fine_tile = fine_map[0]
    coarse = coarse_map[0]
    fine_rows, fine_cols, channels = fine_tile.shape
    coarse_rows, coarse_cols = (coarse.shape[0], coarse.shape[1])

    top_rows = jnp.concatenate([fine_tile[:WIN], coarse[:WIN]], axis=1)
    below_rows = halo_from_next(top_rows, "tile")

    share_feats = first_weight.shape[0]
    feats = share_feats * tile_count
    width = max(
        -(-((t + 1) * share_feats) // 128) - t * share_feats // 128 for t in range(tile_count)
    )
    starts = [min(t * share_feats // 128, feats // 128 - width) for t in range(tile_count)]
    lanes = width * 128
    feat_off = band * share_feats - 128 * jnp.minimum(
        band * share_feats // 128, feats // 128 - width
    )

    first_rows = lax.dynamic_update_slice(
        jnp.zeros((first_weight.shape[1], lanes), jnp.bfloat16),
        first_weight.T,
        (0, feat_off),
    )
    both = lax.all_gather(
        jnp.concatenate([first_rows, second_weight.T], axis=1), "dp", axis=0, tiled=True
    )
    first_all = both[:, :lanes]
    second_all = both[:, lanes:]

    fields = proposal_boxes[0]
    levels = level_plan[0]
    owner = fields[0] // (4 * fine_rows)
    members = (owner[:, None] == jnp.arange(tile_count, dtype=jnp.int32)[None, :]).astype(jnp.int32)
    rank = jnp.sum((jnp.cumsum(members, axis=0) - 1) * members, axis=1)
    relative = lax.rem(owner - band + tile_count, tile_count)
    slot_id = relative * capacity + rank
    slots = tile_count * capacity
    chosen = slot_id[None, :] == jnp.arange(slots, dtype=jnp.int32)[:, None]
    upstream_slots = jnp.dot(
        chosen.astype(jnp.bfloat16), upstream[0], preferred_element_type=jnp.float32
    ).astype(jnp.bfloat16)
    mine = chosen[:capacity].astype(jnp.int32)
    top, left, height, box_width = (
        jnp.sum(mine * fields[f][None, :], axis=1) for f in range(4)
    )
    level = jnp.sum(mine * levels[None, :], axis=1)

    stride = jnp.where(level == 0, 4, 8).astype(jnp.int32)
    is_fine = level == 0
    first_row = top // stride
    local_row = jnp.clip(
        first_row - band * jnp.where(is_fine, fine_rows, coarse_rows),
        0,
        jnp.where(is_fine, fine_rows, coarse_rows) - 1,
    )
    first_col = jnp.minimum(left // stride, jnp.where(is_fine, fine_cols, coarse_cols) - WIN)
    cells = jnp.stack(
        [local_row + jnp.where(is_fine, 0, fine_rows + WIN), first_col], axis=0
    ).astype(jnp.int32)
    stride_float = stride.astype(jnp.float32)
    geo = jnp.stack(
        [
            top.astype(jnp.float32) / stride_float - first_row.astype(jnp.float32),
            height.astype(jnp.float32) / (7.0 * stride_float),
            left.astype(jnp.float32) / stride_float - first_col.astype(jnp.float32),
            box_width.astype(jnp.float32) / (7.0 * stride_float),
        ],
        axis=0,
    )

    side = ((0, 0), (0, fine_cols - coarse_cols), (0, 0))
    maps = jnp.concatenate(
        [
            fine_tile,
            below_rows[:, :fine_cols],
            jnp.pad(coarse, side),
            jnp.pad(below_rows[:, fine_cols:], side),
        ],
        axis=0,
    )
    crop_blocks = make_crops(cells, geo, maps, starts, width, capacity)
    own_feats = jnp.concatenate(
        [
            from_ahead(
                lax.dynamic_index_in_dim(
                    crop_blocks, lax.rem(band - d + tile_count, tile_count), 0, keepdims=False
                ),
                "tile",
                d,
            )
            for d in range(tile_count)
        ],
        axis=0,
    )

    partial_hidden = lax.dot_general(
        own_feats, first_all, (((1,), (1,)), ((), ())), preferred_element_type=jnp.float32
    ).astype(jnp.bfloat16)
    share = second_weight.shape[0]

    def in_my_order(block, d):
        return jnp.roll(block, d * capacity, axis=0) if d else block

    hidden_own = 0.0
    for d in range(tile_count):
        to = lax.rem(band - d + tile_count, tile_count)
        piece = lax.dynamic_slice_in_dim(partial_hidden, to * share, share, axis=1)
        hidden_own = hidden_own + in_my_order(from_ahead(piece, "tile", d), d).astype(jnp.float32)
    gelu_value, gelu_slope = gelu_parts(hidden_own)
    activated = gelu_value.astype(jnp.bfloat16)
    back_grad = jnp.dot(upstream_slots, second_all, preferred_element_type=jnp.float32)
    pre_own = (back_grad * gelu_slope).astype(jnp.bfloat16)
    ahead = [in_my_order(from_ahead(pre_own, "tile", d), d) for d in range(tile_count)]
    twice = jnp.concatenate(ahead + ahead[:-1], axis=1)
    pre_grad = lax.dynamic_slice_in_dim(
        twice, lax.rem(tile_count - band, tile_count) * share, tile_count * share, axis=1
    )
    over_rows = (((0,), (0,)), ((), ()))
    second_part = lax.dot_general(
        upstream_slots, activated, over_rows, preferred_element_type=jnp.float32
    ).astype(jnp.bfloat16)
    first_part = lax.dot_general(
        pre_grad, own_feats, over_rows, preferred_element_type=jnp.float32
    ).astype(jnp.bfloat16)
    summed = lax.psum_scatter(
        jnp.concatenate([first_part, second_part], axis=1), "dp", scatter_dimension=0, tiled=True
    ).astype(jnp.float32)
    first_grad = lax.dynamic_slice_in_dim(summed[:, :lanes], feat_off, share_feats, axis=1).T
    second_grad = summed[:, lanes:].T
    return (first_grad, second_grad)


def solution(mesh):
    placed = (
        P("dp", None, None),
        P("dp", None),
        P("dp", "tile", None, None),
        P("dp", "tile", None, None),
        P("tile", "dp"),
        P("tile", "dp"),
        P("dp", None, None),
    )
    return jax.shard_map(
        per_device,
        mesh=mesh,
        in_specs=placed,
        out_specs=(P("tile", "dp"), P("tile", "dp")),
        check_vma=False,
    )
```
